32 devices in a mesh: ctx: 8 (over z, core), head: 4 (over y, x).
Axes of the slice: x: 2, y: 2, z: 4, core: 2. Of those that a mesh axis runs over, the one named last changes fastest.
Arguments:
- queries: bfloat16 [1024, 8192], P('ctx', 'head'), parts along dimension 1, may hold values from -17 to 17
- keys: bfloat16 [1024, 512], P('ctx', 'head'), parts along dimension 1, may hold values from -17 to 17
- values: bfloat16 [1024, 512], P('ctx', 'head'), parts along dimension 1, may hold values from -6 to 6
- block_position: int32 [8], P('ctx'), may hold values from 0 to 7, each once
Outputs:
- attended: bfloat16 [1024, 8192], P('ctx', 'head'), parts along dimension 1
The draws below stay inside these ranges and needn't reach their ends.
There are 4 independent parts, one for each index of `head`. The reference program is written for one: setup_inputs(seed, part) draws one part's arguments, and reference() takes and returns one part's arrays. A program takes and returns all parts, laid end to end along the dimension named above; an argument that names none is the same for every part. Nothing has to cross between parts.
All inputs are finite; a program needn't handle non-finite values.
Results may differ from the reference program's by a relative error of at most 0.005.
Values may be sent and summed in bfloat16 or wider, within the bound.
No kernel may reach another device: no remote copies, remote signals or barrier semaphores. Data moves between devices by JAX's collectives and lax.ppermute only.
A program may use at most 128 MiB of HBM per device.

```python
import math
import jax
import jax.numpy as jnp
from jax import lax

HEAD_DIM = 128
QHEADS = 16
BLOCK = 128
SEQ = 1024
NBLK = 8


def common(key):
    folded = jax.random.fold_in(key, 11)
    key_query, key_keys = jax.random.split(folded, 2)
    query_draw = jnp.clip(jax.random.normal(key_query, (SEQ, QHEADS, HEAD_DIM), jnp.float32), -6.0, 6.0)
    key_draw = 1.5 * jnp.clip(jax.random.normal(key_keys, (SEQ, HEAD_DIM), jnp.float32), -6.0, 6.0)
    return (query_draw.reshape(SEQ, QHEADS * HEAD_DIM), key_draw)


def draw_queries(key, part):
    return common(key)[0].astype(jnp.bfloat16)


def draw_keys(key, part):
    return common(key)[1].astype(jnp.bfloat16)


def levels(key, dims, cuts, smallest, high):
    def one(dim, shards_of):
        draws = jax.random.uniform(jax.random.fold_in(jax.random.fold_in(key, 6), dim), (shards_of,), jnp.float32, smallest / len(cuts), high / len(cuts))
        return jnp.repeat(jnp.exp(draws), dims[dim] // shards_of).reshape((-1,) + (1,) * (len(dims) - dim - 1))

    gain = one(*cuts[0])
    for cut in cuts[1:]:
        gain = gain * one(*cut)
    return gain


def gaussian(own_key, dims, scale, most, pieces=(), kind=jnp.bfloat16):
    entries = jax.random.normal(own_key, dims, jnp.float32) * scale
    if len(pieces) > 0:
        entries = levels(own_key, dims, pieces, -0.22, 0.18) * entries
    return jnp.clip(entries, min=-most, max=most).astype(kind)


def setup_inputs(seed: int = 0, part: int = 0) -> dict:
    key_of = jax.random.split(jax.random.key(seed), 5)
    part_keys = jax.random.split(jax.random.fold_in(key_of[4], part), 5)
    return {
        "queries": draw_queries(jax.random.fold_in(jax.random.fold_in(key_of[4], part), 71), part),
        "keys": draw_keys(jax.random.fold_in(jax.random.fold_in(key_of[4], part), 71), part),
        "values": gaussian(part_keys[2], (SEQ, HEAD_DIM), 1.0, 6.0, ((0, 8),)),
        "block_position": jax.random.permutation(key_of[3], NBLK).astype(jnp.int32),
    }


def reference(queries, keys, values, block_position):
    row_ids = jnp.arange(SEQ, dtype=jnp.int32)
    position = jnp.take(block_position, row_ids // BLOCK) * BLOCK + row_ids % BLOCK
    query_heads = queries.reshape(SEQ, QHEADS, HEAD_DIM)
    keys_wide = keys.astype(jnp.float32)
    values_wide = values.astype(jnp.float32)
    scale = 1.0 / math.sqrt(HEAD_DIM)
    query_block = math.gcd(SEQ, 512)

    def one_block(block_index):
        first_row = (block_index * query_block).astype(jnp.int32)
        query_rows = lax.dynamic_slice_in_dim(query_heads, first_row, query_block, 0).astype(jnp.float32)
        query_pos = lax.dynamic_slice_in_dim(position, first_row, query_block, 0)
        scores = jnp.einsum('thd,nd->thn', query_rows, keys_wide) * scale
        visible = position[None, None, :] <= query_pos[:, None, None]
        peak = lax.optimization_barrier(jnp.max(jnp.where(visible, scores, -1e+30), axis=-1, keepdims=True))
        weights = jnp.where(visible, jnp.exp(scores - peak), 0.0)
        total = lax.optimization_barrier(jnp.sum(weights, axis=-1, keepdims=True))
        rounded = weights.astype(jnp.bfloat16).astype(jnp.float32)
        output = jnp.einsum('thn,nd->thd', rounded, values_wide) / total
        return output.astype(jnp.bfloat16).reshape(query_block, QHEADS * HEAD_DIM)
    blocks = lax.map(one_block, jnp.arange(SEQ // query_block, dtype=jnp.int32))
    return blocks.reshape(SEQ, QHEADS * HEAD_DIM)
```

```python
import functools
import math

import jax
import jax.numpy as jnp
from jax import lax
from jax.experimental import pallas as pl
from jax.experimental.pallas import tpu as pltpu
from jax.sharding import PartitionSpec as P

HEAD_DIM = 128
QHEADS = 16
BLOCK = 128
CORES = 2
POS_ROWS = 16
PACKET = 2 * BLOCK + POS_ROWS
CHUNK = 2 * BLOCK
LOG2E_SCALE = math.log2(math.e) / math.sqrt(HEAD_DIM)


def attend_kernel(group, pieces, q_ref, mine_ref, other_ref, o_ref, k_all, v_all, m_ref, acc_ref, pos_ref):
    packets = [(ref, i) for ref in (mine_ref, other_ref) for i in range(pieces)]

    @pl.when(pl.program_id(0) == 0)
    def _():
        v_all[:, HEAD_DIM:] = jnp.ones((v_all.shape[0], HEAD_DIM), v_all.dtype)
        for i, (ref, piece) in enumerate(packets):
            base = piece * PACKET
            tag = ref[base + 2 * BLOCK : base + PACKET, :].astype(jnp.float32)
            place = jnp.max(tag).astype(jnp.int32)
            if i == 0:
                pos_ref[0] = place
            rows = pl.ds(pl.multiple_of(place * BLOCK, BLOCK), BLOCK)
            k_all[rows, :] = ref[base : base + BLOCK, :]
            v_all[rows, :HEAD_DIM] = ref[base + BLOCK : base + 2 * BLOCK, :]

    place = pos_ref[0]
    last = place // (CHUNK // BLOCK)

    def scores(head, rows):
        q = q_ref[:, head * HEAD_DIM : (head + 1) * HEAD_DIM]
        return lax.dot_general(
            q, k_all[rows, :], (((1,), (1,)), ((), ())), preferred_element_type=jnp.float32
        )

    rows = pl.ds(pl.multiple_of(last * CHUNK, CHUNK), CHUNK)
    row_id = lax.broadcasted_iota(jnp.int32, (BLOCK, CHUNK), 0) + place * BLOCK
    col_id = lax.broadcasted_iota(jnp.int32, (BLOCK, CHUNK), 1) + last * CHUNK
    visible = col_id <= row_id
    for head in range(group):
        s = jnp.where(visible, scores(head, rows), -1e30)
        m = jnp.max(s, axis=-1, keepdims=True)
        p = jnp.exp2((s - m) * LOG2E_SCALE).astype(jnp.bfloat16)
        acc_ref[head] = jnp.dot(p, v_all[rows, :], preferred_element_type=jnp.float32)
        m_ref[head] = jnp.broadcast_to(m, (BLOCK, HEAD_DIM))

    def step(chunk, carry):
        rows = pl.ds(pl.multiple_of(chunk * CHUNK, CHUNK), CHUNK)
        for head in range(group):
            s = scores(head, rows)
            old = m_ref[head][:, :1]
            m = jnp.maximum(old, jnp.max(s, axis=-1, keepdims=True))
            alpha = jnp.exp2((old - m) * LOG2E_SCALE)
            p = jnp.exp2((s - m) * LOG2E_SCALE).astype(jnp.bfloat16)
            pv = jnp.dot(p, v_all[rows, :], preferred_element_type=jnp.float32)
            acc_ref[head] = acc_ref[head] * alpha + pv
            m_ref[head] = jnp.broadcast_to(m, (BLOCK, HEAD_DIM))
        return carry

    lax.fori_loop(0, last, step, 0)
    for head in range(group):
        acc = acc_ref[head]
        out = acc[:, :HEAD_DIM] / acc[:, HEAD_DIM:]
        o_ref[:, head * HEAD_DIM : (head + 1) * HEAD_DIM] = out.astype(o_ref.dtype)


def attend(queries, mine, other, group=4):
    pieces = mine.shape[0] // PACKET
    total = 2 * pieces * BLOCK
    spec = pl.BlockSpec((BLOCK, group * HEAD_DIM), lambda g: (0, g))
    whole = pl.BlockSpec(mine.shape, lambda g: (0, 0))
    return pl.pallas_call(
        functools.partial(attend_kernel, group, pieces),
        out_shape=jax.ShapeDtypeStruct(queries.shape, queries.dtype),
        grid=(QHEADS // group,),
        in_specs=[spec, whole, whole],
        out_specs=spec,
        scratch_shapes=[
            pltpu.VMEM((total, HEAD_DIM), jnp.bfloat16),
            pltpu.VMEM((total, 2 * HEAD_DIM), jnp.bfloat16),
            pltpu.VMEM((group, BLOCK, HEAD_DIM), jnp.float32),
            pltpu.VMEM((group, BLOCK, 2 * HEAD_DIM), jnp.float32),
            pltpu.SMEM((1,), jnp.int32),
        ],
        compiler_params=pltpu.CompilerParams(vmem_limit_bytes=16 * 2**20),
    )(queries, mine, other)


def body(size, queries, keys, values, block_position):
    tag = jnp.broadcast_to(block_position.astype(jnp.bfloat16)[:, None], (POS_ROWS, HEAD_DIM))
    packet = jnp.concatenate([keys, values, tag], axis=0)
    gathered = [packet]
    for shift in range(CORES, size, CORES):
        pairs = [(i, (i + shift) % size) for i in range(size)]
        gathered.append(lax.ppermute(packet, "ctx", pairs))
    mine = jnp.concatenate(gathered, axis=0)
    other = lax.ppermute(mine, "ctx", [(i, i ^ 1) for i in range(size)])
    return attend(queries, mine, other)


def solution(mesh):
    placed = (P("ctx", "head"), P("ctx", "head"), P("ctx", "head"), P("ctx"))
    return jax.shard_map(
        functools.partial(body, mesh.shape["ctx"]),
        mesh=mesh,
        in_specs=placed,
        out_specs=P("ctx", "head"),
        check_vma=False,
    )
```

```python
import functools
import math

import jax
import jax.numpy as jnp
from jax import lax
from jax.experimental import pallas as pl
from jax.experimental.pallas import tpu as pltpu
from jax.sharding import PartitionSpec as P

HEAD_DIM = 128
QHEADS = 16
BLOCK = 128
CORES = 2
POS_ROWS = 16
PACKET = 2 * BLOCK + POS_ROWS
PAIR = 2 * BLOCK
LOG2E_SCALE = math.log2(math.e) / math.sqrt(HEAD_DIM)
ABT = (((1,), (1,)), ((), ()))


def pack(keys, values, block_position):
    tag = jnp.broadcast_to(block_position.astype(keys.dtype)[:, None], (POS_ROWS, HEAD_DIM))
    return jnp.concatenate([keys, values, tag], axis=0)


def attend_kernel(chunk, unroll, q_ref, mine_ref, other_ref, o_ref, k_all, vt_all, scores, peaks):
    pieces = mine_ref.shape[0] // PACKET
    packets = [(ref, i * PACKET) for ref in (mine_ref, other_ref) for i in range(pieces)]
    count = len(packets)
    total = count * BLOCK
    last = QHEADS // 2 - 1

    vt_all[HEAD_DIM:, :] = jnp.ones((POS_ROWS, total), vt_all.dtype)
    for i, (ref, base) in enumerate(packets):
        k_all[i * BLOCK : (i + 1) * BLOCK, :] = ref[base : base + BLOCK, :]
        vt_all[:HEAD_DIM, i * BLOCK : (i + 1) * BLOCK] = ref[base + BLOCK : base + 2 * BLOCK, :].T

    def place(i):
        ref, base = packets[i]
        tag = ref[base + 2 * BLOCK : base + PACKET, :].astype(jnp.float32)
        return jnp.concatenate([tag[:8], tag[:8]], axis=1)

    own = place(0)
    seen = [None] + [place(i) < own for i in range(1, count)]
    key = lax.broadcasted_iota(jnp.int32, (BLOCK, PAIR), 0)
    row = lax.broadcasted_iota(jnp.int32, (BLOCK, PAIR), 1) % BLOCK
    diagonal = key <= row

    def columns(head):
        if isinstance(head, int):
            return slice(head * HEAD_DIM, (head + 1) * HEAD_DIM)
        return pl.ds(pl.multiple_of(head * HEAD_DIM, HEAD_DIM), HEAD_DIM)

    def pair_queries(pair):
        return jnp.concatenate([q_ref[:, columns(2 * pair + j)] for j in range(2)], axis=0)

    def score(slot, start, q, peak):
        s = lax.dot_general(
            k_all[start : start + chunk, :], q, ABT, preferred_element_type=jnp.float32
        )
        for j in range(chunk // BLOCK):
            i = start // BLOCK + j
            block = s[j * BLOCK : (j + 1) * BLOCK]
            if i == 0:
                block = jnp.where(diagonal, block, -1e30)
            scores[slot, i * BLOCK : (i + 1) * BLOCK, :] = block
            top = block.reshape(BLOCK // 8, 8, PAIR).max(axis=0)
            if i > 0:
                top = jnp.where(seen[i], top, -1e30)
            peak = top if peak is None else jnp.maximum(peak, top)
        return peak

    def weigh(slot, start, peak, acc):
        weights = []
        for j in range(chunk // BLOCK):
            i = start // BLOCK + j
            bound = peak if i == 0 else jnp.where(seen[i], peak, 1e30)
            s = scores[slot, i * BLOCK : (i + 1) * BLOCK, :].reshape(BLOCK // 8, 8, PAIR)
            w = jnp.exp2((s - bound[None]) * LOG2E_SCALE)
            weights.append(w.reshape(BLOCK, PAIR).astype(jnp.bfloat16))
        part = jnp.dot(
            vt_all[:, start : start + chunk],
            jnp.concatenate(weights, axis=0),
            preferred_element_type=jnp.float32,
        )
        return part if acc is None else acc + part

    def keep(slot, peak):
        peaks[slot] = jnp.broadcast_to(peak.max(axis=0, keepdims=True), (8, PAIR))

    def write(pair, acc):
        out = (acc[:HEAD_DIM] / acc[HEAD_DIM : HEAD_DIM + 1]).astype(o_ref.dtype)
        for j in range(2):
            o_ref[:, columns(2 * pair + j)] = out[:, j * BLOCK : (j + 1) * BLOCK].T

    def step(pair, slot, ahead):
        q = pair_queries(pair + 1) if ahead else None
        bound = peaks[slot]
        peak = acc = None
        for start in range(0, total, chunk):
            if ahead:
                peak = score(1 - slot, start, q, peak)
            acc = weigh(slot, start, bound, acc)
        if ahead:
            keep(1 - slot, peak)
        write(pair, acc)

    q, peak = pair_queries(0), None
    for start in range(0, total, chunk):
        peak = score(0, start, q, peak)
    keep(0, peak)
    if unroll:
        for pair in range(last):
            step(pair, pair % 2, True)
    else:

        def two(i, carry):
            step(2 * i, 0, True)
            step(2 * i + 1, 1, True)
            return carry

        lax.fori_loop(0, last // 2, two, 0)
        step(last - 1, 0, True)
    step(last, last % 2, False)


def attend(queries, mine, other):
    total = 2 * (mine.shape[0] // PACKET) * BLOCK
    chunk = math.gcd(total, 8 * BLOCK)
    vmem = pl.BlockSpec(memory_space=pltpu.VMEM)
    return pl.pallas_call(
        functools.partial(attend_kernel, chunk, total == chunk),
        out_shape=jax.ShapeDtypeStruct(queries.shape, queries.dtype),
        in_specs=[vmem] * 3,
        out_specs=vmem,
        scratch_shapes=[
            pltpu.VMEM((total, HEAD_DIM), jnp.bfloat16),
            pltpu.VMEM((HEAD_DIM + POS_ROWS, total), jnp.bfloat16),
            pltpu.VMEM((2, total, PAIR), jnp.float32),
            pltpu.VMEM((2, 8, PAIR), jnp.float32),
        ],
        compiler_params=pltpu.CompilerParams(vmem_limit_bytes=24 * 2**20),
    )(queries, mine, other)


def body(size, queries, keys, values, block_position):
    packet = pack(keys, values, block_position)
    gathered = [packet]
    for shift in range(CORES, size, CORES):
        pairs = [(i, (i + shift) % size) for i in range(size)]
        gathered.append(lax.ppermute(packet, "ctx", pairs))
    mine = jnp.concatenate(gathered, axis=0)
    other = lax.ppermute(mine, "ctx", [(i, i ^ 1) for i in range(size)])
    return attend(queries, mine, other)


def solution(mesh):
    placed = (P("ctx", "head"), P("ctx", "head"), P("ctx", "head"), P("ctx"))
    return jax.shard_map(
        functools.partial(body, mesh.shape["ctx"]),
        mesh=mesh,
        in_specs=placed,
        out_specs=P("ctx", "head"),
        check_vma=False,
    )
```

```python
import functools
import math

import jax
import jax.numpy as jnp
from jax import lax
from jax.experimental import pallas as pl
from jax.experimental.pallas import tpu as pltpu
from jax.sharding import PartitionSpec as P


HEAD_DIM = 128
QHEADS = 16
BLOCK = 128
CORES = 2
POS_ROWS = 16
PACKET = 2 * BLOCK + POS_ROWS
PAIR = 2 * BLOCK
LOG2E_SCALE = math.log2(math.e) / math.sqrt(HEAD_DIM)
ABT = (((1,), (1,)), ((), ()))


def pack(keys, values, block_position):
    tag = jnp.broadcast_to(block_position.astype(keys.dtype)[:, None], (POS_ROWS, HEAD_DIM))
    return jnp.concatenate([keys, values, tag], axis=0)


def stage_kernel(source, target, sem):
    copy = pltpu.make_async_copy(source, target, sem)
    copy.start()
    copy.wait()


def stage(queries):
    return pl.pallas_call(
        stage_kernel,
        out_shape=pltpu.VMEM(queries.shape, queries.dtype),
        in_specs=[pl.BlockSpec(memory_space=pltpu.HBM)],
        out_specs=pl.BlockSpec(memory_space=pltpu.VMEM),
        scratch_shapes=[pltpu.SemaphoreType.DMA],
        compiler_params=pltpu.CompilerParams(vmem_limit_bytes=2**20),
    )(pltpu.with_memory_space_constraint(queries, pltpu.HBM))


def attend_kernel(chunk, unroll, first, final, *refs):
    q_ref, mine_ref, *refs = refs
    keys_ref = mine_ref
    if not first:
        keys_ref, old_acc, old_peak, *refs = refs
    outs, (k_all, vt_all, scores, peaks) = refs[:-4], refs[-4:]
    count = keys_ref.shape[0] // PACKET
    total = count * BLOCK
    last = QHEADS // 2 - 1

    def place(ref, i):
        tag = ref[i * PACKET + 2 * BLOCK : (i + 1) * PACKET, :].astype(jnp.float32)
        return jnp.concatenate([tag[:8], tag[:8]], axis=1)

    vt_all[HEAD_DIM:, :] = jnp.ones((POS_ROWS, total), vt_all.dtype)
    for i in range(count):
        base = i * PACKET
        rows = slice(i * BLOCK, (i + 1) * BLOCK)
        k_all[rows, :] = keys_ref[base : base + BLOCK, :]
        vt_all[:HEAD_DIM, rows] = keys_ref[base + BLOCK : base + 2 * BLOCK, :].T

    own = place(mine_ref, 0)
    seen = [None if first and i == 0 else place(keys_ref, i) < own for i in range(count)]
    key = lax.broadcasted_iota(jnp.int32, (BLOCK, PAIR), 0)
    row = lax.broadcasted_iota(jnp.int32, (BLOCK, PAIR), 1) % BLOCK
    diagonal = key <= row

    def columns(head):
        if isinstance(head, int):
            return slice(head * HEAD_DIM, (head + 1) * HEAD_DIM)
        return pl.ds(pl.multiple_of(head * HEAD_DIM, HEAD_DIM), HEAD_DIM)

    def pair_queries(pair):
        return jnp.concatenate([q_ref[:, columns(2 * pair + j)] for j in range(2)], axis=0)

    def score(slot, start, q, peak):
        s = lax.dot_general(
            k_all[start : start + chunk, :], q, ABT, preferred_element_type=jnp.float32
        )
        for j in range(chunk // BLOCK):
            i = start // BLOCK + j
            block = s[j * BLOCK : (j + 1) * BLOCK]
            if seen[i] is None:
                block = jnp.where(diagonal, block, -1e30)
            scores[slot, i * BLOCK : (i + 1) * BLOCK, :] = block
            top = block.reshape(BLOCK // 8, 8, PAIR).max(axis=0)
            if seen[i] is not None:
                top = jnp.where(seen[i], top, -1e30)
            peak = top if peak is None else jnp.maximum(peak, top)
        return peak

    def weigh(slot, start, peak, acc):
        weights = []
        for j in range(chunk // BLOCK):
            i = start // BLOCK + j
            bound = peak if seen[i] is None else jnp.where(seen[i], peak, 1e30)
            s = scores[slot, i * BLOCK : (i + 1) * BLOCK, :].reshape(BLOCK // 8, 8, PAIR)
            w = jnp.exp2((s - bound[None]) * LOG2E_SCALE)
            weights.append(w.reshape(BLOCK, PAIR).astype(jnp.bfloat16))
        part = jnp.dot(
            vt_all[:, start : start + chunk],
            jnp.concatenate(weights, axis=0),
            preferred_element_type=jnp.float32,
        )
        return part if acc is None else acc + part

    def keep(pair, slot, peak):
        peak = jnp.broadcast_to(peak.max(axis=0, keepdims=True), (8, PAIR))
        if not first:
            peak = jnp.maximum(peak, old_peak[pair])
        if not final:
            outs[1][pair] = peak
        peaks[slot] = peak

    def write(pair, acc, peak):
        if not first:
            alpha = jnp.exp2((old_peak[pair] - peak) * LOG2E_SCALE)
            old = old_acc[pair].reshape(-1, 8, PAIR) * alpha[None]
            acc = acc + old.reshape(acc.shape)
        if not final:
            outs[0][pair] = acc
            return
        out = (acc[:HEAD_DIM] / acc[HEAD_DIM : HEAD_DIM + 1]).astype(outs[0].dtype)
        for j in range(2):
            outs[0][:, columns(2 * pair + j)] = out[:, j * BLOCK : (j + 1) * BLOCK].T

    def step(pair, slot, ahead):
        q = pair_queries(pair + 1) if ahead else None
        bound = peaks[slot]
        peak = acc = None
        for start in range(0, total, chunk):
            if ahead:
                peak = score(1 - slot, start, q, peak)
            acc = weigh(slot, start, bound, acc)
        if ahead:
            keep(pair + 1, 1 - slot, peak)
        write(pair, acc, bound)

    q, peak = pair_queries(0), None
    for start in range(0, total, chunk):
        peak = score(0, start, q, peak)
    keep(0, 0, peak)
    if unroll:
        for pair in range(last):
            step(pair, pair % 2, True)
    else:

        def two(i, carry):
            step(2 * i, 0, True)
            step(2 * i + 1, 1, True)
            return carry

        lax.fori_loop(0, last // 2, two, 0)
        step(last - 1, 0, True)
    step(last, last % 2, False)


def attend(queries, mine, state, keys, final):
    total = keys.shape[0] // PACKET * BLOCK
    chunk = math.gcd(total, 4 * BLOCK)
    vmem = pl.BlockSpec(memory_space=pltpu.VMEM)
    args = (queries, mine) if state is None else (queries, mine, keys, *state)
    shapes = (
        jax.ShapeDtypeStruct((QHEADS // 2, HEAD_DIM + POS_ROWS, PAIR), jnp.float32),
        jax.ShapeDtypeStruct((QHEADS // 2, 8, PAIR), jnp.float32),
    )
    return pl.pallas_call(
        functools.partial(attend_kernel, chunk, total == chunk, state is None, final),
        out_shape=jax.ShapeDtypeStruct(queries.shape, queries.dtype) if final else shapes,
        in_specs=[vmem] * len(args),
        out_specs=vmem if final else (vmem, vmem),
        scratch_shapes=[
            pltpu.VMEM((total, HEAD_DIM), jnp.bfloat16),
            pltpu.VMEM((HEAD_DIM + POS_ROWS, total), jnp.bfloat16),
            pltpu.VMEM((2, total, PAIR), jnp.float32),
            pltpu.VMEM((2, 8, PAIR), jnp.float32),
        ],
        compiler_params=pltpu.CompilerParams(vmem_limit_bytes=24 * 2**20),
    )(*args)


def body(size, queries, keys, values, block_position):
    packet = lax.optimization_barrier(pack(keys, values, block_position))
    arrived = []
    for shift in range(size - CORES, 0, -CORES):
        pairs = [(i, (i + shift) % size) for i in range(size)]
        arrived.append(lax.ppermute(packet, "ctx", pairs))
    queries = stage(queries)
    arrived.append(packet)
    arrived.reverse()
    half = len(arrived) // 2
    state = mine = None
    for name, group in (("near", arrived[:half]), ("far", arrived[half:])):
        group = jnp.concatenate(group, axis=0)
        mine = group if mine is None else mine
        partner = lax.ppermute(group, "ctx", [(i, i ^ 1) for i in range(size)])
        state = attend(queries, mine, state, group, False)
        state = attend(queries, mine, state, partner, name == "far")
    return state


def solution(mesh):
    placed = (P("ctx", "head"), P("ctx", "head"), P("ctx", "head"), P("ctx"))
    return jax.shard_map(
        functools.partial(body, mesh.shape["ctx"]),
        mesh=mesh,
        in_specs=placed,
        out_specs=P("ctx", "head"),
        check_vma=False,
    )
```

```python
import functools
import math

import jax
import jax.numpy as jnp
from jax import lax
from jax.experimental import pallas as pl
from jax.experimental.pallas import tpu as pltpu
from jax.sharding import PartitionSpec as P


HEAD_DIM = 128
QHEADS = 16
BLOCK = 128
CORES = 2
POS_ROWS = 16
PACKET = 2 * BLOCK + POS_ROWS
PAIR = 2 * BLOCK
LOG2E_SCALE = math.log2(math.e) / math.sqrt(HEAD_DIM)
ABT = (((1,), (1,)), ((), ()))


def pack_kernel(k_ref, v_ref, place_ref, packet_ref, sems):
    copies = [
        pltpu.make_async_copy(ref, packet_ref.at[pl.ds(i * BLOCK, BLOCK)], sems.at[i])
        for i, ref in enumerate((k_ref, v_ref))
    ]
    for copy in copies:
        copy.start()
    place = jnp.full((POS_ROWS, HEAD_DIM), place_ref[0], jnp.int32)
    packet_ref[2 * BLOCK :, :] = place.astype(jnp.float32).astype(packet_ref.dtype)
    for copy in copies:
        copy.wait()


def in_hbm(array):
    return pltpu.with_memory_space_constraint(array, pltpu.HBM)


HBM_SPEC = pl.BlockSpec(memory_space=pltpu.HBM)
VMEM_SPEC = pl.BlockSpec(memory_space=pltpu.VMEM)


def pack(keys, values, block_position):
    return pl.pallas_call(
        pack_kernel,
        out_shape=pltpu.VMEM((PACKET, HEAD_DIM), keys.dtype),
        in_specs=[HBM_SPEC, HBM_SPEC, pl.BlockSpec(memory_space=pltpu.SMEM)],
        out_specs=VMEM_SPEC,
        scratch_shapes=[pltpu.SemaphoreType.DMA((2,))],
        compiler_params=pltpu.CompilerParams(vmem_limit_bytes=2**20),
    )(in_hbm(keys), in_hbm(values), block_position)


def attend_kernel(chunk, unroll, first, final, *refs):
    q_ref, mine_ref, *refs = refs
    keys_ref = mine_ref
    if not first:
        keys_ref, old_acc, old_peak, *refs = refs
    *refs, k_all, vt_all, scores, peaks = refs
    if first:
        acc_ref, peak_ref, q_here, sems = refs
    elif final:
        o_ref, o_here, sems = refs
    else:
        acc_ref, peak_ref = refs
    count = keys_ref.shape[0] // PACKET
    total = count * BLOCK
    last = QHEADS // 2 - 1

    def place(ref, i):
        tag = ref[i * PACKET + 2 * BLOCK : (i + 1) * PACKET, :].astype(jnp.float32)
        return jnp.concatenate([tag[:8], tag[:8]], axis=1)

    own = place(mine_ref, 0)
    seen = [None if first and i == 0 else place(keys_ref, i) < own for i in range(count)]
    key = lax.broadcasted_iota(jnp.int32, (BLOCK, PAIR), 0)
    row = lax.broadcasted_iota(jnp.int32, (BLOCK, PAIR), 1) % BLOCK
    diagonal = key <= row

    def columns(index, width):
        if isinstance(index, int):
            return pl.ds(index * width, width)
        return pl.ds(pl.multiple_of(index * width, width), width)

    def moved(pair):
        cols = columns(pair, 2 * HEAD_DIM)
        source, target = (q_ref, q_here) if first else (o_here, o_ref)
        return pltpu.make_async_copy(source.at[:, cols], target.at[:, cols], sems.at[pair])

    def pair_queries(pair):
        source = q_ref
        if first:
            moved(pair).wait()
            source = q_here
        heads = [source[:, columns(2 * pair + j, HEAD_DIM)] for j in range(2)]
        return jnp.concatenate(heads, axis=0)

    if first:
        for pair in range(last + 1):
            moved(pair).start()

    vt_all[HEAD_DIM:, :] = jnp.ones((POS_ROWS, total), vt_all.dtype)
    for i in range(count):
        base = i * PACKET
        rows = slice(i * BLOCK, (i + 1) * BLOCK)
        k_all[rows, :] = keys_ref[base : base + BLOCK, :]
        vt_all[:HEAD_DIM, rows] = keys_ref[base + BLOCK : base + 2 * BLOCK, :].T

    def score(slot, start, q, peak):
        s = lax.dot_general(
            k_all[start : start + chunk, :], q, ABT, preferred_element_type=jnp.float32
        )
        for j in range(chunk // BLOCK):
            i = start // BLOCK + j
            block = s[j * BLOCK : (j + 1) * BLOCK]
            if seen[i] is None:
                block = jnp.where(diagonal, block, -1e30)
            scores[slot, i * BLOCK : (i + 1) * BLOCK, :] = block
            top = block.reshape(BLOCK // 8, 8, PAIR).max(axis=0)
            if seen[i] is not None:
                top = jnp.where(seen[i], top, -1e30)
            peak = top if peak is None else jnp.maximum(peak, top)
        return peak

    def weigh(slot, start, peak, acc):
        weights = []
        for j in range(chunk // BLOCK):
            i = start // BLOCK + j
            bound = peak if seen[i] is None else jnp.where(seen[i], peak, 1e30)
            s = scores[slot, i * BLOCK : (i + 1) * BLOCK, :].reshape(BLOCK // 8, 8, PAIR)
            w = jnp.exp2((s - bound[None]) * LOG2E_SCALE)
            weights.append(w.reshape(BLOCK, PAIR).astype(jnp.bfloat16))
        part = jnp.dot(
            vt_all[:, start : start + chunk],
            jnp.concatenate(weights, axis=0),
            preferred_element_type=jnp.float32,
        )
        return part if acc is None else acc + part

    def keep(pair, slot, peak):
        peak = jnp.broadcast_to(peak.max(axis=0, keepdims=True), (8, PAIR))
        if not first:
            peak = jnp.maximum(peak, old_peak[pair])
        if not final:
            peak_ref[pair] = peak
        peaks[slot] = peak

    def write(pair, acc, peak):
        if not first:
            alpha = jnp.exp2((old_peak[pair] - peak) * LOG2E_SCALE)
            old = old_acc[pair].reshape(-1, 8, PAIR) * alpha[None]
            acc = acc + old.reshape(acc.shape)
        if not final:
            acc_ref[pair] = acc
            return
        out = (acc[:HEAD_DIM] / acc[HEAD_DIM : HEAD_DIM + 1]).astype(o_here.dtype)
        for j in range(2):
            o_here[:, columns(2 * pair + j, HEAD_DIM)] = out[:, j * BLOCK : (j + 1) * BLOCK].T
        moved(pair).start()

    def step(pair, slot, ahead):
        q = pair_queries(pair + 1) if ahead else None
        bound = peaks[slot]
        peak = acc = None
        for start in range(0, total, chunk):
            if ahead:
                peak = score(1 - slot, start, q, peak)
            acc = weigh(slot, start, bound, acc)
        if ahead:
            keep(pair + 1, 1 - slot, peak)
        write(pair, acc, bound)

    q, peak = pair_queries(0), None
    for start in range(0, total, chunk):
        peak = score(0, start, q, peak)
    keep(0, 0, peak)
    if unroll:
        for pair in range(last):
            step(pair, pair % 2, True)
    else:

        def two(i, carry):
            step(2 * i, 0, True)
            step(2 * i + 1, 1, True)
            return carry

        lax.fori_loop(0, last // 2, two, 0)
        step(last - 1, 0, True)
    step(last, last % 2, False)
    if final:
        for pair in range(last + 1):
            moved(pair).wait()


def attend(queries, mine, state, keys, final):
    first = state is None
    total = keys.shape[0] // PACKET * BLOCK
    chunk = math.gcd(total, 4 * BLOCK)
    pairs = QHEADS // 2
    args = (in_hbm(queries), mine) if first else (queries, mine, keys, *state)
    in_specs = [HBM_SPEC if first else VMEM_SPEC] + [VMEM_SPEC] * (len(args) - 1)
    scratch = [
        pltpu.VMEM((total, HEAD_DIM), jnp.bfloat16),
        pltpu.VMEM((HEAD_DIM + POS_ROWS, total), jnp.bfloat16),
        pltpu.VMEM((2, total, PAIR), jnp.float32),
        pltpu.VMEM((2, 8, PAIR), jnp.float32),
    ]
    if final:
        shapes = jax.ShapeDtypeStruct(queries.shape, queries.dtype)
        out_specs = HBM_SPEC
        scratch = [pltpu.VMEM(queries.shape, queries.dtype), pltpu.SemaphoreType.DMA((pairs,))] + scratch
    else:
        shapes = [
            pltpu.VMEM((pairs, HEAD_DIM + POS_ROWS, PAIR), jnp.float32),
            pltpu.VMEM((pairs, 8, PAIR), jnp.float32),
        ]
        if first:
            shapes.append(pltpu.VMEM(queries.shape, queries.dtype))
            scratch = [pltpu.SemaphoreType.DMA((pairs,))] + scratch
        out_specs = [VMEM_SPEC] * len(shapes)
    return pl.pallas_call(
        functools.partial(attend_kernel, chunk, total == chunk, first, final),
        out_shape=shapes,
        in_specs=in_specs,
        out_specs=out_specs,
        scratch_shapes=scratch,
        compiler_params=pltpu.CompilerParams(vmem_limit_bytes=24 * 2**20),
    )(*args)


def body(size, queries, keys, values, block_position):
    packet = pack(keys, values, block_position)
    arrived = []
    for shift in range(size - CORES, 0, -CORES):
        pairs = [(i, (i + shift) % size) for i in range(size)]
        arrived.append(lax.ppermute(packet, "ctx", pairs))
    arrived.append(packet)
    arrived.reverse()
    half = len(arrived) // 2
    state = mine = None
    for name, group in (("near", arrived[:half]), ("far", arrived[half:])):
        group = jnp.concatenate(group, axis=0)
        mine = group if mine is None else mine
        partner = lax.ppermute(group, "ctx", [(i, i ^ 1) for i in range(size)])
        state = attend(queries, mine, state, group, False)
        if name == "near":
            *state, queries = state
        state = attend(queries, mine, state, partner, name == "far")
    return state


def solution(mesh):
    placed = (P("ctx", "head"), P("ctx", "head"), P("ctx", "head"), P("ctx"))
    return jax.shard_map(
        functools.partial(body, mesh.shape["ctx"]),
        mesh=mesh,
        in_specs=placed,
        out_specs=P("ctx", "head"),
        check_vma=False,
    )
```

```python
import functools
import math

import jax
import jax.numpy as jnp
from jax import lax
from jax.experimental import pallas as pl
from jax.experimental.pallas import tpu as pltpu
from jax.sharding import PartitionSpec as P


HEAD_DIM = 128
QHEADS = 16
BLOCK = 128
CORES = 2
POS_ROWS = 16
PACKET = 2 * BLOCK + POS_ROWS
PARTS = 2
PAIR = 2 * BLOCK
LOG2E_SCALE = math.log2(math.e) / math.sqrt(HEAD_DIM)
ABT = (((1,), (1,)), ((), ()))


def ones_kernel(ones_ref):
    ones_ref[...] = jnp.ones(ones_ref.shape, ones_ref.dtype)


def tag_kernel(place_ref, ones_ref, tag_ref):
    tag_ref[...] = (ones_ref[...] * place_ref[0].astype(jnp.float32)).astype(tag_ref.dtype)


def pack_kernel(k_ref, v_ref, tag_ref, packet_ref):
    packet_ref[:BLOCK, :] = k_ref[...]
    packet_ref[BLOCK : 2 * BLOCK, :] = v_ref[...].T
    packet_ref[2 * BLOCK :, :] = tag_ref[...]


VMEM_SPEC = pl.BlockSpec(memory_space=pltpu.VMEM)
SLOW = pl.CostEstimate(flops=2**40, bytes_accessed=2**14, transcendentals=0)
SMALL = pltpu.CompilerParams(vmem_limit_bytes=2**20)


def pack(keys, values, block_position):
    ones = pl.pallas_call(
        ones_kernel,
        out_shape=pltpu.VMEM((POS_ROWS, HEAD_DIM), jnp.float32),
        out_specs=VMEM_SPEC,
        compiler_params=SMALL,
        cost_estimate=SLOW,
    )()
    block_position, ones = lax.optimization_barrier((block_position, ones))
    tag = pl.pallas_call(
        tag_kernel,
        out_shape=pltpu.VMEM((POS_ROWS, HEAD_DIM), keys.dtype),
        in_specs=[pl.BlockSpec(memory_space=pltpu.SMEM), VMEM_SPEC],
        out_specs=VMEM_SPEC,
        compiler_params=SMALL,
    )(block_position, ones)
    return pl.pallas_call(
        pack_kernel,
        out_shape=pltpu.VMEM((PACKET, HEAD_DIM), keys.dtype),
        in_specs=[VMEM_SPEC] * 3,
        out_specs=VMEM_SPEC,
        compiler_params=SMALL,
    )(keys, values, tag)


def attend_kernel(chunk, unroll, first, final, *refs):
    q_ref, mine_ref, *refs = refs
    keys_ref = mine_ref
    if not first:
        keys_ref, old_acc, old_peak, *refs = refs
    outs, (k_all, vt_all, scores, peaks) = refs[:-4], refs[-4:]
    if final:
        o_ref, *outs, sems = outs

        def leave(part):
            width = o_ref.shape[1] // PARTS
            cols = pl.ds(part * width, width)
            return pltpu.make_async_copy(outs[0].at[:, cols], o_ref.at[:, cols], sems.at[part])
    count = keys_ref.shape[0] // PACKET
    total = count * BLOCK
    last = QHEADS // 2 - 1

    def place(ref, i):
        tag = ref[i * PACKET + 2 * BLOCK : (i + 1) * PACKET, :].astype(jnp.float32)
        return jnp.concatenate([tag[:8], tag[:8]], axis=1)

    vt_all[HEAD_DIM:, :] = jnp.ones((POS_ROWS, total), vt_all.dtype)
    for i in range(count):
        base = i * PACKET
        rows = slice(i * BLOCK, (i + 1) * BLOCK)
        k_all[rows, :] = keys_ref[base : base + BLOCK, :]
        vt_all[:HEAD_DIM, rows] = keys_ref[base + BLOCK : base + 2 * BLOCK, :]

    own = place(mine_ref, 0)
    seen = [None if first and i == 0 else place(keys_ref, i) < own for i in range(count)]
    key = lax.broadcasted_iota(jnp.int32, (BLOCK, PAIR), 0)
    row = lax.broadcasted_iota(jnp.int32, (BLOCK, PAIR), 1) % BLOCK
    diagonal = key <= row

    def columns(head):
        if isinstance(head, int):
            return slice(head * HEAD_DIM, (head + 1) * HEAD_DIM)
        return pl.ds(pl.multiple_of(head * HEAD_DIM, HEAD_DIM), HEAD_DIM)

    def pair_queries(pair):
        return jnp.concatenate([q_ref[:, columns(2 * pair + j)] for j in range(2)], axis=0)

    def score(slot, start, q, peak):
        s = lax.dot_general(
            k_all[start : start + chunk, :], q, ABT, preferred_element_type=jnp.float32
        )
        for j in range(chunk // BLOCK):
            i = start // BLOCK + j
            block = s[j * BLOCK : (j + 1) * BLOCK]
            if seen[i] is None:
                block = jnp.where(diagonal, block, -1e30)
            scores[slot, i * BLOCK : (i + 1) * BLOCK, :] = block
            top = block.reshape(BLOCK // 8, 8, PAIR).max(axis=0)
            if seen[i] is not None:
                top = jnp.where(seen[i], top, -1e30)
            peak = top if peak is None else jnp.maximum(peak, top)
        return peak

    def weigh(slot, start, peak, acc):
        weights = []
        for j in range(chunk // BLOCK):
            i = start // BLOCK + j
            bound = peak if seen[i] is None else jnp.where(seen[i], peak, 1e30)
            s = scores[slot, i * BLOCK : (i + 1) * BLOCK, :].reshape(BLOCK // 8, 8, PAIR)
            w = jnp.exp2((s - bound[None]) * LOG2E_SCALE)
            weights.append(w.reshape(BLOCK, PAIR).astype(jnp.bfloat16))
        part = jnp.dot(
            vt_all[:, start : start + chunk],
            jnp.concatenate(weights, axis=0),
            preferred_element_type=jnp.float32,
        )
        return part if acc is None else acc + part

    def keep(pair, slot, peak):
        peak = jnp.broadcast_to(peak.max(axis=0, keepdims=True), (8, PAIR))
        if not first:
            peak = jnp.maximum(peak, old_peak[pair])
        if not final:
            outs[1][pair] = peak
        peaks[slot] = peak

    def write(pair, acc, peak):
        if not first:
            alpha = jnp.exp2((old_peak[pair] - peak) * LOG2E_SCALE)
            old = old_acc[pair].reshape(-1, 8, PAIR) * alpha[None]
            acc = acc + old.reshape(acc.shape)
        if not final:
            outs[0][pair] = acc
            return
        inverse = 1.0 / acc[HEAD_DIM : HEAD_DIM + 8]
        out = acc[:HEAD_DIM].reshape(HEAD_DIM // 8, 8, PAIR) * inverse[None]
        out = out.reshape(HEAD_DIM, PAIR).astype(outs[0].dtype)
        for j in range(2):
            outs[0][:, columns(2 * pair + j)] = out[:, j * BLOCK : (j + 1) * BLOCK].T

    def step(pair, slot, ahead):
        q = pair_queries(pair + 1) if ahead else None
        bound = peaks[slot]
        peak = acc = None
        for start in range(0, total, chunk):
            if ahead:
                peak = score(1 - slot, start, q, peak)
            acc = weigh(slot, start, bound, acc)
        if ahead:
            keep(pair + 1, 1 - slot, peak)
        write(pair, acc, bound)

    q, peak = pair_queries(0), None
    for start in range(0, total, chunk):
        peak = score(0, start, q, peak)
    keep(0, 0, peak)
    if unroll:
        for pair in range(last):
            step(pair, pair % 2, True)
            if final and (pair + 1) * PARTS % (last + 1) == 0:
                leave((pair + 1) * PARTS // (last + 1) - 1).start()
    else:

        def two(i, carry):
            step(2 * i, 0, True)
            step(2 * i + 1, 1, True)
            return carry

        lax.fori_loop(0, last // 2, two, 0)
        step(last - 1, 0, True)
        if final:
            for part in range(PARTS - 1):
                leave(part).start()
    step(last, last % 2, False)
    if final:
        leave(PARTS - 1).start()
        for part in range(PARTS):
            leave(part).wait()


def attend(queries, mine, state, keys, final):
    total = keys.shape[0] // PACKET * BLOCK
    chunk = math.gcd(total, 4 * BLOCK)
    vmem = pl.BlockSpec(memory_space=pltpu.VMEM)
    args = (queries, mine) if state is None else (queries, mine, keys, *state)
    leaving = []
    if final:
        leaving = [pltpu.VMEM(queries.shape, queries.dtype), pltpu.SemaphoreType.DMA((PARTS,))]
    shapes = (
        jax.ShapeDtypeStruct((QHEADS // 2, HEAD_DIM + POS_ROWS, PAIR), jnp.float32),
        jax.ShapeDtypeStruct((QHEADS // 2, 8, PAIR), jnp.float32),
    )
    return pl.pallas_call(
        functools.partial(attend_kernel, chunk, total == chunk, state is None, final),
        out_shape=jax.ShapeDtypeStruct(queries.shape, queries.dtype) if final else shapes,
        in_specs=[vmem] * len(args),
        out_specs=pl.BlockSpec(memory_space=pltpu.HBM) if final else (vmem, vmem),
        scratch_shapes=leaving
        + [
            pltpu.VMEM((total, HEAD_DIM), jnp.bfloat16),
            pltpu.VMEM((HEAD_DIM + POS_ROWS, total), jnp.bfloat16),
            pltpu.VMEM((2, total, PAIR), jnp.float32),
            pltpu.VMEM((2, 8, PAIR), jnp.float32),
        ],
        compiler_params=pltpu.CompilerParams(vmem_limit_bytes=24 * 2**20),
    )(*args)


def body(size, queries, keys, values, block_position):
    packet = pack(keys, values, block_position)
    arrived = []
    for shift in range(size - CORES, 0, -CORES):
        pairs = [(i, (i + shift) % size) for i in range(size)]
        arrived.append(lax.ppermute(packet, "ctx", pairs))
    arrived.append(packet)
    arrived.reverse()
    half = len(arrived) // 2
    state = mine = None
    for name, group in (("near", arrived[:half]), ("far", arrived[half:])):
        group = jnp.concatenate(group, axis=0)
        mine = group if mine is None else mine
        partner = lax.ppermute(group, "ctx", [(i, i ^ 1) for i in range(size)])
        state = attend(queries, mine, state, group, False)
        state = attend(queries, mine, state, partner, name == "far")
    return state


def solution(mesh):
    placed = (P("ctx", "head"), P("ctx", "head"), P("ctx", "head"), P("ctx"))
    return jax.shard_map(
        functools.partial(body, mesh.shape["ctx"]),
        mesh=mesh,
        in_specs=placed,
        out_specs=P("ctx", "head"),
        check_vma=False,
    )
```

```python
import functools
import math

import jax
import jax.numpy as jnp
from jax import lax
from jax.experimental import pallas as pl
from jax.experimental.pallas import tpu as pltpu
from jax.sharding import PartitionSpec as P


HEAD_DIM = 128
QHEADS = 16
BLOCK = 128
CORES = 2
POS_ROWS = 16
PACKET = 2 * BLOCK + POS_ROWS
PARTS = 2
PAIR = 2 * BLOCK
LOG2E_SCALE = math.log2(math.e) / math.sqrt(HEAD_DIM)
ABT = (((1,), (1,)), ((), ()))


def ones_kernel(ones_ref):
    ones_ref[...] = jnp.ones(ones_ref.shape, ones_ref.dtype)


def tag_kernel(place_ref, ones_ref, tag_ref):
    tag_ref[...] = (ones_ref[...] * place_ref[0].astype(jnp.float32)).astype(tag_ref.dtype)


def pack_kernel(k_ref, v_ref, tag_ref, packet_ref):
    packet_ref[:BLOCK, :] = k_ref[...]
    packet_ref[BLOCK : 2 * BLOCK, :] = v_ref[...].T
    packet_ref[2 * BLOCK :, :] = tag_ref[...]


VMEM_SPEC = pl.BlockSpec(memory_space=pltpu.VMEM)
SLOW = pl.CostEstimate(flops=2**40, bytes_accessed=2**14, transcendentals=0)
SMALL = pltpu.CompilerParams(vmem_limit_bytes=2**20)


def pack(keys, values, block_position):
    ones = pl.pallas_call(
        ones_kernel,
        out_shape=pltpu.VMEM((POS_ROWS, HEAD_DIM), jnp.float32),
        out_specs=VMEM_SPEC,
        compiler_params=SMALL,
        cost_estimate=SLOW,
    )()
    block_position, ones = lax.optimization_barrier((block_position, ones))
    tag = pl.pallas_call(
        tag_kernel,
        out_shape=pltpu.VMEM((POS_ROWS, HEAD_DIM), keys.dtype),
        in_specs=[pl.BlockSpec(memory_space=pltpu.SMEM), VMEM_SPEC],
        out_specs=VMEM_SPEC,
        compiler_params=SMALL,
    )(block_position, ones)
    return pl.pallas_call(
        pack_kernel,
        out_shape=pltpu.VMEM((PACKET, HEAD_DIM), keys.dtype),
        in_specs=[VMEM_SPEC] * 3,
        out_specs=VMEM_SPEC,
        compiler_params=SMALL,
    )(keys, values, tag)


def attend_kernel(chunk, unroll, first, final, *refs):
    q_ref, mine_ref, *refs = refs
    keys_ref = mine_ref
    if not first:
        keys_ref, old_acc, old_peak, *refs = refs
    outs, (k_all, vt_all, scores, peaks) = refs[:-4], refs[-4:]
    if final:
        o_ref, *outs, sems = outs

        def leave(part):
            width = o_ref.shape[1] // PARTS
            cols = pl.ds(part * width, width)
            return pltpu.make_async_copy(outs[0].at[:, cols], o_ref.at[:, cols], sems.at[part])
    count = keys_ref.shape[0] // PACKET
    total = count * BLOCK
    last = QHEADS // 2 - 1

    def place(ref, i):
        tag = ref[i * PACKET + 2 * BLOCK : (i + 1) * PACKET, :].astype(jnp.float32)
        return jnp.concatenate([tag[:8], tag[:8]], axis=1)

    vt_all[HEAD_DIM:, :] = jnp.ones((POS_ROWS, total), vt_all.dtype)
    for i in range(count):
        base = i * PACKET
        rows = slice(i * BLOCK, (i + 1) * BLOCK)
        k_all[rows, :] = keys_ref[base : base + BLOCK, :]
        vt_all[:HEAD_DIM, rows] = keys_ref[base + BLOCK : base + 2 * BLOCK, :]

    own = place(mine_ref, 0)
    seen = [None if first and i == 0 else place(keys_ref, i) < own for i in range(count)]
    key = lax.broadcasted_iota(jnp.int32, (BLOCK, PAIR), 0)
    row = lax.broadcasted_iota(jnp.int32, (BLOCK, PAIR), 1) % BLOCK
    diagonal = key <= row

    def columns(head):
        if isinstance(head, int):
            return slice(head * HEAD_DIM, (head + 1) * HEAD_DIM)
        return pl.ds(pl.multiple_of(head * HEAD_DIM, HEAD_DIM), HEAD_DIM)

    def pair_queries(pair):
        return jnp.concatenate([q_ref[:, columns(2 * pair + j)] for j in range(2)], axis=0)

    def score(slot, start, q, peak):
        s = lax.dot_general(
            k_all[start : start + chunk, :], q, ABT, preferred_element_type=jnp.float32
        )
        for j in range(chunk // BLOCK):
            i = start // BLOCK + j
            block = s[j * BLOCK : (j + 1) * BLOCK]
            if seen[i] is None:
                block = jnp.where(diagonal, block, -1e30)
            scores[slot, i * BLOCK : (i + 1) * BLOCK, :] = block
            top = block.reshape(BLOCK // 8, 8, PAIR).max(axis=0)
            if seen[i] is not None:
                top = jnp.where(seen[i], top, -1e30)
            peak = top if peak is None else jnp.maximum(peak, top)
        return peak

    def weigh(slot, start, peak, acc):
        weights = []
        for j in range(chunk // BLOCK):
            i = start // BLOCK + j
            bound = peak if seen[i] is None else jnp.where(seen[i], peak, 1e30)
            s = scores[slot, i * BLOCK : (i + 1) * BLOCK, :].reshape(BLOCK // 8, 8, PAIR)
            w = jnp.exp2((s - bound[None]) * LOG2E_SCALE)
            weights.append(w.reshape(BLOCK, PAIR).astype(jnp.bfloat16))
        part = jnp.dot(
            vt_all[:, start : start + chunk],
            jnp.concatenate(weights, axis=0),
            preferred_element_type=jnp.float32,
        )
        return part if acc is None else acc + part

    def keep(pair, slot, peak):
        peak = jnp.broadcast_to(peak.max(axis=0, keepdims=True), (8, PAIR))
        if not first:
            peak = jnp.maximum(peak, old_peak[pair])
        if not final:
            outs[1][pair] = peak
        peaks[slot] = peak

    def write(pair, acc, peak):
        if not first:
            alpha = jnp.exp2((old_peak[pair] - peak) * LOG2E_SCALE)
            old = old_acc[pair].reshape(-1, 8, PAIR) * alpha[None]
            acc = acc + old.reshape(acc.shape)
        if not final:
            outs[0][pair] = acc
            return
        inverse = 1.0 / acc[HEAD_DIM : HEAD_DIM + 8]
        out = acc[:HEAD_DIM].reshape(HEAD_DIM // 8, 8, PAIR) * inverse[None]
        out = out.reshape(HEAD_DIM, PAIR).astype(outs[0].dtype)
        for j in range(2):
            outs[0][:, columns(2 * pair + j)] = out[:, j * BLOCK : (j + 1) * BLOCK].T

    depth = scores.shape[0] - 1

    def step(pair, slot, ahead):
        q = pair_queries(pair + depth) if ahead else None
        there = (slot + depth) % (depth + 1)
        bound = peaks[slot]
        peak = acc = None
        for start in range(0, total, chunk):
            if ahead:
                peak = score(there, start, q, peak)
            acc = weigh(slot, start, bound, acc)
        if ahead:
            keep(pair + depth, there, peak)
        write(pair, acc, bound)

    for pair in range(depth):
        q, peak = pair_queries(pair), None
        for start in range(0, total, chunk):
            peak = score(pair, start, q, peak)
        keep(pair, pair, peak)
    if unroll:
        for pair in range(last + 1):
            step(pair, pair % (depth + 1), pair + depth <= last)
            if final and pair < last and (pair + 1) * PARTS % (last + 1) == 0:
                leave((pair + 1) * PARTS // (last + 1) - 1).start()
    else:

        def two(i, carry):
            step(2 * i, 0, True)
            step(2 * i + 1, 1, True)
            return carry

        lax.fori_loop(0, last // 2, two, 0)
        step(last - 1, 0, True)
        if final:
            for part in range(PARTS - 1):
                leave(part).start()
        step(last, last % 2, False)
    if final:
        leave(PARTS - 1).start()
        for part in range(PARTS):
            leave(part).wait()


def attend(queries, mine, state, keys, final):
    total = keys.shape[0] // PACKET * BLOCK
    chunk = math.gcd(total, 4 * BLOCK)
    depth = 8 if total == chunk else 1
    vmem = pl.BlockSpec(memory_space=pltpu.VMEM)
    args = (queries, mine) if state is None else (queries, mine, keys, *state)
    leaving = []
    if final:
        leaving = [pltpu.VMEM(queries.shape, queries.dtype), pltpu.SemaphoreType.DMA((PARTS,))]
    shapes = (
        jax.ShapeDtypeStruct((QHEADS // 2, HEAD_DIM + POS_ROWS, PAIR), jnp.float32),
        jax.ShapeDtypeStruct((QHEADS // 2, 8, PAIR), jnp.float32),
    )
    return pl.pallas_call(
        functools.partial(attend_kernel, chunk, total == chunk, state is None, final),
        out_shape=jax.ShapeDtypeStruct(queries.shape, queries.dtype) if final else shapes,
        in_specs=[vmem] * len(args),
        out_specs=pl.BlockSpec(memory_space=pltpu.HBM) if final else (vmem, vmem),
        scratch_shapes=leaving
        + [
            pltpu.VMEM((total, HEAD_DIM), jnp.bfloat16),
            pltpu.VMEM((HEAD_DIM + POS_ROWS, total), jnp.bfloat16),
            pltpu.VMEM((depth + 1, total, PAIR), jnp.float32),
            pltpu.VMEM((depth + 1, 8, PAIR), jnp.float32),
        ],
        compiler_params=pltpu.CompilerParams(vmem_limit_bytes=24 * 2**20),
    )(*args)


def body(size, queries, keys, values, block_position):
    packet = pack(keys, values, block_position)
    arrived = []
    for shift in range(size - CORES, 0, -CORES):
        pairs = [(i, (i + shift) % size) for i in range(size)]
        arrived.append(lax.ppermute(packet, "ctx", pairs))
    arrived.append(packet)
    arrived.reverse()
    half = len(arrived) // 2
    state = mine = None
    for name, group in (("near", arrived[:half]), ("far", arrived[half:])):
        group = jnp.concatenate(group, axis=0)
        mine = group if mine is None else mine
        partner = lax.ppermute(group, "ctx", [(i, i ^ 1) for i in range(size)])
        state = attend(queries, mine, state, group, False)
        state = attend(queries, mine, state, partner, name == "far")
    return state


def solution(mesh):
    placed = (P("ctx", "head"), P("ctx", "head"), P("ctx", "head"), P("ctx"))
    return jax.shard_map(
        functools.partial(body, mesh.shape["ctx"]),
        mesh=mesh,
        in_specs=placed,
        out_specs=P("ctx", "head"),
        check_vma=False,
    )
```

```python
import functools
import math

import jax
import jax.numpy as jnp
from jax import lax
from jax.experimental import pallas as pl
from jax.experimental.pallas import tpu as pltpu
from jax.sharding import PartitionSpec as P


HEAD_DIM = 128
QHEADS = 16
BLOCK = 128
CORES = 2
ONES_ROWS = 16
TAG_ROWS = 8
PACKET = 2 * BLOCK + TAG_ROWS
PARTS = 4
PAIR = 2 * BLOCK
LOG2E_SCALE = math.log2(math.e) / math.sqrt(HEAD_DIM)
ABT = (((1,), (1,)), ((), ()))


def ones_kernel(ones_ref):
    ones_ref[...] = jnp.ones(ones_ref.shape, ones_ref.dtype)


def tag_kernel(place_ref, ones_ref, tag_ref):
    tag_ref[...] = (ones_ref[...] * place_ref[0].astype(jnp.float32)).astype(tag_ref.dtype)


def pack_kernel(k_ref, v_ref, tag_ref, packet_ref):
    packet_ref[:BLOCK, :] = k_ref[...]
    packet_ref[BLOCK : 2 * BLOCK, :] = v_ref[...].T
    packet_ref[2 * BLOCK :, :] = tag_ref[...]


VMEM_SPEC = pl.BlockSpec(memory_space=pltpu.VMEM)
SLOW = pl.CostEstimate(flops=2**40, bytes_accessed=2**14, transcendentals=0)
SMALL = pltpu.CompilerParams(vmem_limit_bytes=2**20)


def pack(keys, values, block_position):
    ones = pl.pallas_call(
        ones_kernel,
        out_shape=pltpu.VMEM((TAG_ROWS, HEAD_DIM), jnp.float32),
        out_specs=VMEM_SPEC,
        compiler_params=SMALL,
        cost_estimate=SLOW,
    )()
    block_position, ones = lax.optimization_barrier((block_position, ones))
    tag = pl.pallas_call(
        tag_kernel,
        out_shape=pltpu.VMEM((TAG_ROWS, HEAD_DIM), keys.dtype),
        in_specs=[pl.BlockSpec(memory_space=pltpu.SMEM), VMEM_SPEC],
        out_specs=VMEM_SPEC,
        compiler_params=SMALL,
    )(block_position, ones)
    return pl.pallas_call(
        pack_kernel,
        out_shape=pltpu.VMEM((PACKET, HEAD_DIM), keys.dtype),
        in_specs=[VMEM_SPEC] * 3,
        out_specs=VMEM_SPEC,
        compiler_params=SMALL,
    )(keys, values, tag)


def attend_kernel(chunk, unroll, first, final, *refs):
    q_ref, mine_ref, *refs = refs
    keys_ref = mine_ref
    if not first:
        keys_ref, old_acc, old_peak, *refs = refs
    outs, (k_all, vt_all, scores, peaks) = refs[:-4], refs[-4:]
    if final:
        o_ref, *outs, sems = outs

        def leave(part):
            width = o_ref.shape[1] // PARTS
            cols = pl.ds(part * width, width)
            return pltpu.make_async_copy(outs[0].at[:, cols], o_ref.at[:, cols], sems.at[part])
    count = keys_ref.shape[0] // PACKET
    total = count * BLOCK
    last = QHEADS // 2 - 1

    def place(ref, i):
        tag = ref[i * PACKET + 2 * BLOCK : (i + 1) * PACKET, :].astype(jnp.float32)
        return jnp.concatenate([tag[:8], tag[:8]], axis=1)

    vt_all[HEAD_DIM:, :] = jnp.ones((ONES_ROWS, total), vt_all.dtype)
    for i in range(count):
        base = i * PACKET
        rows = slice(i * BLOCK, (i + 1) * BLOCK)
        k_all[rows, :] = keys_ref[base : base + BLOCK, :]
        vt_all[:HEAD_DIM, rows] = keys_ref[base + BLOCK : base + 2 * BLOCK, :]

    own = place(mine_ref, 0)
    seen = [None if first and i == 0 else place(keys_ref, i) < own for i in range(count)]
    key = lax.broadcasted_iota(jnp.int32, (BLOCK, PAIR), 0)
    row = lax.broadcasted_iota(jnp.int32, (BLOCK, PAIR), 1) % BLOCK
    diagonal = key <= row

    def columns(head):
        if isinstance(head, int):
            return slice(head * HEAD_DIM, (head + 1) * HEAD_DIM)
        return pl.ds(pl.multiple_of(head * HEAD_DIM, HEAD_DIM), HEAD_DIM)

    def pair_queries(pair):
        return jnp.concatenate([q_ref[:, columns(2 * pair + j)] for j in range(2)], axis=0)

    def score(slot, start, q, peak):
        s = lax.dot_general(
            k_all[start : start + chunk, :], q, ABT, preferred_element_type=jnp.float32
        )
        for j in range(chunk // BLOCK):
            i = start // BLOCK + j
            block = s[j * BLOCK : (j + 1) * BLOCK]
            if seen[i] is None:
                block = jnp.where(diagonal, block, -1e30)
            scores[slot, i * BLOCK : (i + 1) * BLOCK, :] = block
            top = block.reshape(BLOCK // 8, 8, PAIR).max(axis=0)
            if seen[i] is not None:
                top = jnp.where(seen[i], top, -1e30)
            peak = top if peak is None else jnp.maximum(peak, top)
        return peak

    def weigh(slot, start, peak, acc):
        weights = []
        for j in range(chunk // BLOCK):
            i = start // BLOCK + j
            bound = peak if seen[i] is None else jnp.where(seen[i], peak, 1e30)
            s = scores[slot, i * BLOCK : (i + 1) * BLOCK, :].reshape(BLOCK // 8, 8, PAIR)
            w = jnp.exp2((s - bound[None]) * LOG2E_SCALE)
            weights.append(w.reshape(BLOCK, PAIR).astype(jnp.bfloat16))
        part = jnp.dot(
            vt_all[:, start : start + chunk],
            jnp.concatenate(weights, axis=0),
            preferred_element_type=jnp.float32,
        )
        return part if acc is None else acc + part

    def keep(pair, slot, peak):
        peak = jnp.broadcast_to(peak.max(axis=0, keepdims=True), (8, PAIR))
        if not first:
            peak = jnp.maximum(peak, old_peak[pair])
        if not final:
            outs[1][pair] = peak
        peaks[slot] = peak

    def write(pair, acc, peak):
        if not first:
            alpha = jnp.exp2((old_peak[pair] - peak) * LOG2E_SCALE)
            old = old_acc[pair].reshape(-1, 8, PAIR) * alpha[None]
            acc = acc + old.reshape(acc.shape)
        if not final:
            outs[0][pair] = acc
            return
        inverse = 1.0 / acc[HEAD_DIM : HEAD_DIM + 8]
        out = acc[:HEAD_DIM].reshape(HEAD_DIM // 8, 8, PAIR) * inverse[None]
        out = out.reshape(HEAD_DIM, PAIR).astype(outs[0].dtype)
        for j in range(2):
            outs[0][:, columns(2 * pair + j)] = out[:, j * BLOCK : (j + 1) * BLOCK].T

    depth = scores.shape[0] - 1

    def step(pair, slot, ahead):
        q = pair_queries(pair + depth) if ahead else None
        there = (slot + depth) % (depth + 1)
        bound = peaks[slot]
        peak = acc = None
        for start in range(0, total, chunk):
            if ahead:
                peak = score(there, start, q, peak)
            acc = weigh(slot, start, bound, acc)
        if ahead:
            keep(pair + depth, there, peak)
        write(pair, acc, bound)

    for pair in range(depth):
        q, peak = pair_queries(pair), None
        for start in range(0, total, chunk):
            peak = score(pair, start, q, peak)
        keep(pair, pair, peak)
    if unroll:
        for pair in range(last + 1):
            step(pair, pair % (depth + 1), pair + depth <= last)
            if final and pair < last and (pair + 1) * PARTS % (last + 1) == 0:
                leave((pair + 1) * PARTS // (last + 1) - 1).start()
    else:

        def two(i, carry):
            step(2 * i, 0, True)
            step(2 * i + 1, 1, True)
            return carry

        lax.fori_loop(0, last // 2, two, 0)
        step(last - 1, 0, True)
        if final:
            for part in range(PARTS - 1):
                leave(part).start()
        step(last, last % 2, False)
    if final:
        leave(PARTS - 1).start()
        for part in range(PARTS):
            leave(part).wait()


def attend(queries, mine, state, keys, final):
    total = keys.shape[0] // PACKET * BLOCK
    chunk = math.gcd(total, 4 * BLOCK)
    depth = 8 if total == chunk else 1
    vmem = pl.BlockSpec(memory_space=pltpu.VMEM)
    args = (queries, mine) if state is None else (queries, mine, keys, *state)
    leaving = []
    if final:
        leaving = [pltpu.VMEM(queries.shape, queries.dtype), pltpu.SemaphoreType.DMA((PARTS,))]
    shapes = (
        jax.ShapeDtypeStruct((QHEADS // 2, HEAD_DIM + ONES_ROWS, PAIR), jnp.float32),
        jax.ShapeDtypeStruct((QHEADS // 2, 8, PAIR), jnp.float32),
    )
    return pl.pallas_call(
        functools.partial(attend_kernel, chunk, total == chunk, state is None, final),
        out_shape=jax.ShapeDtypeStruct(queries.shape, queries.dtype) if final else shapes,
        in_specs=[vmem] * len(args),
        out_specs=pl.BlockSpec(memory_space=pltpu.HBM) if final else (vmem, vmem),
        scratch_shapes=leaving
        + [
            pltpu.VMEM((total, HEAD_DIM), jnp.bfloat16),
            pltpu.VMEM((HEAD_DIM + ONES_ROWS, total), jnp.bfloat16),
            pltpu.VMEM((depth + 1, total, PAIR), jnp.float32),
            pltpu.VMEM((depth + 1, 8, PAIR), jnp.float32),
        ],
        compiler_params=pltpu.CompilerParams(vmem_limit_bytes=24 * 2**20),
    )(*args)


def body(size, queries, keys, values, block_position):
    packet = pack(keys, values, block_position)
    arrived = []
    for shift in range(size - CORES, 0, -CORES):
        pairs = [(i, (i + shift) % size) for i in range(size)]
        arrived.append(lax.ppermute(packet, "ctx", pairs))
    arrived.append(packet)
    arrived.reverse()
    half = len(arrived) // 2
    state = mine = None
    for name, group in (("near", arrived[:half]), ("far", arrived[half:])):
        group = jnp.concatenate(group, axis=0)
        mine = group if mine is None else mine
        partner = lax.ppermute(group, "ctx", [(i, i ^ 1) for i in range(size)])
        state = attend(queries, mine, state, group, False)
        state = attend(queries, mine, state, partner, name == "far")
    return state


def solution(mesh):
    placed = (P("ctx", "head"), P("ctx", "head"), P("ctx", "head"), P("ctx"))
    return jax.shard_map(
        functools.partial(body, mesh.shape["ctx"]),
        mesh=mesh,
        in_specs=placed,
        out_specs=P("ctx", "head"),
        check_vma=False,
    )
```
